32 devices in a mesh: wrow: 16 (over z, y, x), kblk: 2 (over core).
Axes of the slice: x: 2, y: 2, z: 4, core: 2. Of those that a mesh axis runs over, the one named last changes fastest.
Arguments:
- conduction: bfloat16 [2, 4, 64, 16384], P('kblk', None, None, 'wrow'), may hold values from -6 to 6
- valence: bfloat16 [2, 4, 64, 16384], P(None, None, 'wrow', 'kblk'), may hold values from -6 to 6
- screened: bfloat16 [4, 16384, 16384], P(None, 'wrow', 'kblk'), may hold values from -0.00036621094 to 0.00036621094
- pair_block: int32 [2, 4], replicated, may hold values from 0 to 3, as said below
Outputs:
- kernel: float32 [2, 64, 256], P('kblk', 'wrow')
The draws below stay inside these ranges and needn't reach their ends.
Inputs may be any that keep to these rules, and one draw needn't show every extreme that they name: `pair_block`: every one of the 4 blocks is selected by at least one pair and by at most 3 pairs; one block by exactly 3 pairs.
All inputs are finite; a program needn't handle non-finite values.
Results may differ from the reference program's by a relative error of at most 0.0029.
Values may be sent and summed in bfloat16 or wider, within the bound.
No kernel may reach another device: no remote copies, remote signals or barrier semaphores. Data moves between devices by JAX's collectives and lax.ppermute only.
A program may use at most 128 MiB of HBM per device.

```python
import jax
import jax.numpy as jnp
from jax import lax

NG = 16384
C = 8
V = 8
KP = 4
NQ = 4
NK = 2
CAP = 3
SLAB = 8192


def draw_pair_block(key, part):
    total = NK * KP
    key_full = jax.random.fold_in(key, 11)
    key_shift = jax.random.fold_in(key, 12)
    key_perm = jax.random.fold_in(key, 13)
    full_block = jax.random.randint(key_full, (), 0, NQ)
    shift = jax.random.randint(key_shift, (), 0, NQ - 1)
    positions = jnp.arange(total, dtype=jnp.int32)
    others = (positions - CAP + shift) % (NQ - 1)
    others = jnp.where(others >= full_block, others + 1, others)
    labels = jnp.where(positions < CAP, full_block, others)
    labels = jax.random.permutation(key_perm, labels)
    return labels.reshape(NK, KP).astype(jnp.int32)


def block_levels(key, shape, shards, low, high):
    def one(position, parts):
        draws = jax.random.uniform(jax.random.fold_in(jax.random.fold_in(key, 6), position), (parts,), jnp.float32, low / len(shards), high / len(shards))
        return jnp.repeat(jnp.exp(draws), shape[position] // parts).reshape((-1,) + (1,) * (len(shape) - position - 1))

    factor_of = one(*shards[0])
    for cut in shards[1:]:
        factor_of = factor_of * one(*cut)
    return factor_of


def centred(stream_key, shape, deviation, reach, pieces=(), kind=jnp.bfloat16):
    drawn = jax.random.normal(stream_key, shape, jnp.float32) * deviation
    if len(pieces) > 0:
        drawn = block_levels(stream_key, shape, pieces, -0.22, 0.18) * drawn
    return jnp.clip(drawn, min=-reach, max=reach).astype(kind)


def setup_inputs(seed: int = 0) -> dict:
    keys = jax.random.split(jax.random.key(seed), 5)
    conduction = centred(keys[0], (NK, KP, C * C, NG), 1.0, 6.0, ((0, 2), (3, 16)))
    valence = centred(keys[1], (NK, KP, V * V, NG), 1.0, 6.0, ((2, 16), (3, 2)))
    screened = centred(keys[2], (NQ, NG, NG), (NG * NG) ** -0.5, 0.00036621094, ((1, 16), (2, 2)))
    pair_block = draw_pair_block(jax.random.fold_in(keys[4], 71), 0)
    return dict(conduction=conduction, valence=valence, screened=screened, pair_block=pair_block)


def reference(conduction, valence, screened, pair_block):
    pair_count = NK * KP
    cond_rows = conduction.reshape(pair_count, C * C, NG)
    vale_rows = valence.reshape(pair_count, V * V, NG)
    blocks = pair_block.reshape(pair_count).astype(jnp.int32)
    slab_count = NG // SLAB

    def one_pair(items):
        cond_one, vale_one, block = items
        w_full = lax.dynamic_index_in_dim(screened, block, 0, keepdims=False)

        def one_slab(total, slab):
            start = (slab * SLAB).astype(jnp.int32)
            w_cols = lax.dynamic_slice_in_dim(w_full, start, SLAB, 1)
            v_cols = lax.dynamic_slice_in_dim(vale_one, start, SLAB, 1)
            part = jnp.dot(v_cols, w_cols.T, preferred_element_type=jnp.float32).astype(jnp.bfloat16)
            return total + jnp.dot(cond_one, part.T, preferred_element_type=jnp.float32), None

        total, _ = lax.scan(one_slab, jnp.zeros((C * C, V * V), jnp.float32), jnp.arange(slab_count, dtype=jnp.int32))
        return total

    tiles = lax.map(one_pair, (cond_rows, vale_rows, blocks))
    tiles = tiles.reshape(NK, KP, C, C, V, V).transpose(0, 2, 4, 1, 3, 5)
    return tiles.reshape(NK, C * V, KP * C * V)
```

```python
import functools

import jax
import jax.numpy as jnp
from jax import lax
from jax.experimental import pallas as pl
from jax.experimental.pallas import tpu as pltpu
from jax.sharding import PartitionSpec as P


C = 8
V = 8
AXES = ("wrow", "kblk")
GROUP = 3
PIECES = 8


def pairs_of(n, m, move):
    return [(w * m + c, move(w, c) * m + c) for w in range(n) for c in range(m)]


def move(array, n, m, to):
    return lax.ppermute(array, AXES, pairs_of(n, m, to))


def gather_valence(own, n, m):
    to_a = lambda w, c: w ^ (1 if c % 2 == 0 else 2)
    to_b = lambda w, c: w ^ (2 if c % 2 == 0 else 1)
    near, far = (lambda w, c: w ^ 4), (lambda z: lambda w, c: w ^ (4 * z))
    base = [own]
    for z in range(1, n // 4):
        if z % 2 == 0:
            base.append(move(own, n, m, far(z)))
        else:
            base.append(move(base[z - 1], n, m, near))
    in_a, in_b, in_ab = [], [], []
    for z in range(n // 4):
        if z == 1:
            in_a.append(move(in_a[0], n, m, near))
            in_ab.append(move(in_ab[0], n, m, near))
        else:
            in_a.append(move(base[z], n, m, to_a))
            in_ab.append(move(in_a[z], n, m, to_b))
        in_b.append(move(base[z], n, m, to_b))
    return [slot for four in zip(base, in_a, in_b, in_ab) for slot in four]


def project_kernel(cap, kp, blocks, me, cond, w, *refs):
    x, lhs, slot = refs[-3:]
    q, t = pl.program_id(0), pl.program_id(1)
    pair_count, comps, _ = cond.shape
    width = w.shape[2]

    @pl.when(t == 0)
    def _():
        count = jnp.int32(0)
        for p in range(pair_count):
            match = blocks[p // kp, p % kp] == q

            @pl.when(match)
            def _():
                source = ((p // kp) ^ me[0]) * kp + p % kp
                lhs[count] = cond[source]
                slot[count] = p

            count = count + match.astype(jnp.int32)
        slot[cap] = count

    left = slot[cap]
    columns = pl.ds(pl.multiple_of(t * width, width), width)
    for first in range(0, cap, GROUP):
        for size in range(1, min(GROUP, cap - first) + 1):
            last = size == min(GROUP, cap - first)
            here = (left - first >= size) if last else (left - first == size)

            @pl.when(here)
            def _():
                rows = lhs[first : first + size].reshape(size * comps, lhs.shape[2])
                part = jnp.dot(rows, w[0], preferred_element_type=jnp.float32)
                for s in range(size):
                    x[slot[first + s], :, columns] = part[s * comps : (s + 1) * comps].astype(x.dtype)


def project(piece, pieces, kp, blocks, me, cond, screened):
    pair_count, comps, rows = cond.shape
    block_count, _, cols = screened.shape
    cap = 3 * pair_count // 8
    span = cols // pieces
    tile = min(1024, span)
    steps = span // tile
    return pl.pallas_call(
        functools.partial(project_kernel, cap, kp),
        out_shape=jax.ShapeDtypeStruct((pair_count, comps, span), cond.dtype),
        grid_spec=pltpu.PrefetchScalarGridSpec(
            num_scalar_prefetch=2,
            grid=(block_count, steps),
            in_specs=[
                pl.BlockSpec((pair_count, comps, rows), lambda q, t, *_: (0, 0, 0)),
                pl.BlockSpec((1, rows, tile), lambda q, t, *_: (q, 0, piece * steps + t)),
            ],
            out_specs=pl.BlockSpec((pair_count, comps, span), lambda q, t, *_: (0, 0, 0)),
            scratch_shapes=[
                pltpu.VMEM((cap, comps, rows), cond.dtype),
                pltpu.SMEM((cap + 1,), jnp.int32),
            ],
        ),
        compiler_params=pltpu.CompilerParams(vmem_limit_bytes=16 << 20),
        cost_estimate=pl.CostEstimate(
            flops=2 * pair_count * comps * rows * span,
            bytes_accessed=2 * (block_count * rows * span + pair_count * comps * (rows + span)),
            transcendentals=0,
        ),
        name="project",
    )(blocks, me, cond, screened)


def contract_kernel(kp, parts, n, row_of, col_of, *refs):
    xs, vale = refs[: -n - 1], refs[-n - 1 : -1]
    out = refs[-1]
    comps, width = xs[0].shape[1:]
    k_count = xs[0].shape[0] // kp
    rows = vale[0].shape[0] // k_count
    total = n * rows
    local = rows // kp
    index = lax.broadcasted_iota(jnp.int32, (total, total), 0)
    slot, inner = index // rows, index % rows
    swapped = (slot // 4) * 4 + (slot % 2) * 2 + (slot // 2) % 2
    comp = (jnp.where(col_of[0] % 2 == 0, slot, swapped) ^ row_of[0]) * local + inner % local
    lanes = total // parts
    size = lanes // kp
    target = (comp // size) * lanes + (inner // local) * size + comp % size
    order = (target == lax.broadcasted_iota(jnp.int32, (total, total), 1)).astype(jnp.float32)
    of_kp = (lax.broadcasted_iota(jnp.int32, (comps, total), 1) // local) % kp

    picked = []
    for k in range(k_count):
        acc = jnp.zeros((kp * comps, total), jnp.float32)
        for t, x in enumerate(xs):
            left = x[k * kp : (k + 1) * kp].reshape(kp * comps, width)
            right = jnp.concatenate([v[k * rows : (k + 1) * rows, t * width : (t + 1) * width] for v in vale], axis=0)
            acc += lax.dot_general(left, right, (((1,), (1,)), ((), ())), preferred_element_type=jnp.float32)
        one = jnp.zeros((comps, total), jnp.float32)
        for j in range(kp):
            one = jnp.where(of_kp == j, acc[j * comps : (j + 1) * comps], one)
        picked.append(one)
    ordered = jnp.dot(
        jnp.concatenate(picked, axis=0),
        order,
        precision=lax.Precision.HIGHEST,
        preferred_element_type=jnp.float32,
    )
    for k in range(k_count):
        for c in range(C):
            for part in range(parts):
                row = k * comps + c * C
                out[c * parts + part, k] = ordered[row : row + C, part * lanes : (part + 1) * lanes]


def contract(kp, k_count, parts, row, col, xs, slots):
    pair_count, comps, _ = xs[0].shape
    rows, cols = slots[0].shape
    n = len(slots)
    total = n * rows // k_count
    return pl.pallas_call(
        functools.partial(contract_kernel, kp, parts, n),
        out_shape=jax.ShapeDtypeStruct((C * parts, k_count, C, total // parts), jnp.float32),
        in_specs=[pl.BlockSpec(memory_space=pltpu.SMEM)] * 2 + [pl.BlockSpec(memory_space=pltpu.VMEM)] * (len(xs) + n),
        out_specs=pl.BlockSpec(memory_space=pltpu.VMEM),
        compiler_params=pltpu.CompilerParams(vmem_limit_bytes=32 << 20),
        cost_estimate=pl.CostEstimate(
            flops=2 * pair_count * comps * total * cols,
            bytes_accessed=2 * cols * (pair_count * comps + n * rows),
            transcendentals=0,
        ),
        name="contract",
    )(row, col, *xs, *slots)


def per_device(n, m, *args):
    return direct_kernel(n, m, *args)


def direct_kernel(n, m, conduction, valence, screened, pair_block):
    k_count, kp = pair_block.shape
    comps = conduction.shape[2]
    pair_count = k_count * kp
    local = valence.shape[2]
    cols = valence.shape[3]
    w = lax.axis_index("wrow").astype(jnp.int32)
    c = lax.axis_index("kblk").astype(jnp.int32)

    conds = [conduction]
    for i in range(1, m):
        conds.append(lax.ppermute(conduction, AXES, [(a * m + b, a * m + (b ^ i)) for a in range(n) for b in range(m)]))
    own = valence.reshape(pair_count * local, cols)
    cond = jnp.concatenate(conds, axis=0).reshape(pair_count, comps, conduction.shape[3])
    me = (c * (k_count // m)).reshape(1)

    slots = gather_valence(own, n, m)
    xs = []
    for piece in range(PIECES):
        xs.append(project(piece, PIECES, kp, pair_block, me, cond, screened))

    parts = n // C
    width = V * V // parts
    mine = contract(kp, k_count, parts, w.reshape(1), c.reshape(1), xs, slots)

    sent = mine.reshape(n * k_count, C, kp * width)
    got = lax.all_to_all(sent, AXES, 0, 0, tiled=True)
    total = got.reshape(n * m, k_count // m, C, kp, width // V, V).sum(0)
    return total.transpose(0, 3, 2, 1, 4).reshape(k_count // m, width // V, kp * C * V)


def solution(mesh):
    n, m = mesh.shape["wrow"], mesh.shape["kblk"]
    return jax.shard_map(
        functools.partial(per_device, n, m),
        mesh=mesh,
        in_specs=(
            P("kblk", None, None, "wrow"),
            P(None, None, "wrow", "kblk"),
            P(None, "wrow", "kblk"),
            P(),
        ),
        out_specs=P("kblk", "wrow", None),
        check_vma=False,
    )
```

```python
import functools

import jax
import jax.numpy as jnp
from jax import lax
from jax.experimental import pallas as pl
from jax.experimental.pallas import tpu as pltpu
from jax.sharding import PartitionSpec as P


C = 8
V = 8
AXES = ("wrow", "kblk")
GROUP = 3
PIECES = 4
AHEAD = 4


def pairs_of(n, m, to, across):
    return [(w * m + c, to(w, c) * m + across(c)) for w in range(n) for c in range(m)]


def move(array, n, m, to, across=lambda c: c):
    return lax.ppermute(array, AXES, pairs_of(n, m, to, across))


def gather_valence(own, n, m):
    to_a = lambda w, c: w ^ (1 if c % 2 == 0 else 2)
    to_b = lambda w, c: w ^ (2 if c % 2 == 0 else 1)
    near, far = (lambda w, c: w ^ 4), (lambda z: lambda w, c: w ^ (4 * z))
    base = [own]
    for z in range(1, n // 4):
        if z % 2 == 0:
            base.append(move(own, n, m, far(z)))
        else:
            base.append(move(base[z - 1], n, m, near))
    in_a, in_b, in_ab = [], [], []
    for z in range(n // 4):
        if z == 1:
            in_a.append(move(in_a[0], n, m, near))
            in_ab.append(move(in_ab[0], n, m, near))
        else:
            in_a.append(move(base[z], n, m, to_a))
            in_ab.append(move(in_a[z], n, m, to_b))
        in_b.append(move(base[z], n, m, to_b))
    return [slot for four in zip(base, in_a, in_b, in_ab) for slot in four]


def project_kernel(cap, kp, piece, blocks, me, row_of, cond, w, x, lhs, slot, tiles, arrived):
    pair_count, comps, _ = cond.shape
    block_count, _, span = tiles.shape
    halves = arrived.shape[1]
    width = span // halves

    def fetch(q, half):
        return pltpu.make_async_copy(
            w.at[q, :, pl.ds(piece * span + half * width, width)],
            tiles.at[q, :, pl.ds(half * width, width)],
            arrived.at[q, half],
        )

    for i in range(AHEAD):
        fetch(i // halves, i % halves).start()

    @pl.loop(0, block_count)
    def _(q):
        count = jnp.int32(0)
        for p in range(pair_count):
            match = blocks[p // kp, p % kp] == q

            @pl.when(match)
            def _():
                lhs[count] = cond[((p // kp) ^ me[0]) * kp + p % kp]
                slot[count] = p

            count = count + match.astype(jnp.int32)
        for half in range(halves):
            columns = pl.ds(half * width, width)
            fetch(q, half).wait()
            later, part_of = (half + AHEAD) // halves, (half + AHEAD) % halves

            @pl.when(q + later < block_count)
            def _():
                fetch(q + later, part_of).start()

            for first in range(0, cap, GROUP):
                size = min(GROUP, cap - first)

                @pl.when(count > first)
                def _():
                    rows = lhs[first : first + size].reshape(size * comps, lhs.shape[2])
                    part = jnp.dot(rows, tiles[q, :, columns], preferred_element_type=jnp.float32).astype(x.dtype)
                    for s in range(size):

                        @pl.when(count > first + s)
                        def _():
                            x[slot[first + s], :, columns] = part[s * comps : (s + 1) * comps]


def project(piece, pieces, kp, blocks, me, row_of, cond, screened):
    pair_count, comps, rows = cond.shape
    block_count, _, cols = screened.shape
    cap = 3 * pair_count // 8
    span = cols // pieces
    halves = 2
    return pl.pallas_call(
        functools.partial(project_kernel, cap, kp, piece),
        out_shape=jax.ShapeDtypeStruct((pair_count, comps, span), cond.dtype),
        in_specs=[
            pl.BlockSpec(memory_space=pltpu.SMEM),
            pl.BlockSpec(memory_space=pltpu.SMEM),
            pl.BlockSpec(memory_space=pltpu.SMEM),
            pl.BlockSpec(memory_space=pltpu.VMEM),
            pl.BlockSpec(memory_space=pl.ANY),
        ],
        out_specs=pl.BlockSpec(memory_space=pltpu.VMEM),
        scratch_shapes=[
            pltpu.VMEM((cap, comps, rows), cond.dtype),
            pltpu.SMEM((cap,), jnp.int32),
            pltpu.VMEM((block_count, rows, span), screened.dtype),
            pltpu.SemaphoreType.DMA((block_count, halves)),
        ],
        compiler_params=pltpu.CompilerParams(vmem_limit_bytes=24 << 20),
        cost_estimate=pl.CostEstimate(
            flops=2 * pair_count * comps * rows * span,
            bytes_accessed=2 * (block_count * rows * span + pair_count * comps * (rows + span)),
            transcendentals=0,
        ),
        name="project",
    )(blocks, me, row_of, cond, screened)


def contract_kernel(kp, parts, n, row_of, col_of, *refs):
    xs, vale = refs[: -n - 1], refs[-n - 1 : -1]
    out = refs[-1]
    comps, width = xs[0].shape[1:]
    k_count = xs[0].shape[0] // kp
    rows = vale[0].shape[0] // k_count
    total = n * rows
    local = rows // kp
    index = lax.broadcasted_iota(jnp.int32, (total, total), 0)
    slot, inner = index // rows, index % rows
    swapped = (slot // 4) * 4 + (slot % 2) * 2 + (slot // 2) % 2
    comp = (jnp.where(col_of[0] % 2 == 0, slot, swapped) ^ row_of[0]) * local + inner % local
    lanes = total // parts
    size = lanes // kp
    target = (comp // size) * lanes + (inner // local) * size + comp % size
    order = (target == lax.broadcasted_iota(jnp.int32, (total, total), 1)).astype(jnp.float32)
    of_kp = (lax.broadcasted_iota(jnp.int32, (comps, total), 1) // local) % kp

    picked = []
    for k in range(k_count):
        acc = jnp.zeros((kp * comps, total), jnp.float32)
        for t, x in enumerate(xs):
            left = x[k * kp : (k + 1) * kp].reshape(kp * comps, width)
            right = jnp.concatenate([v[k * rows : (k + 1) * rows, t * width : (t + 1) * width] for v in vale], axis=0)
            acc += lax.dot_general(left, right, (((1,), (1,)), ((), ())), preferred_element_type=jnp.float32)
        one = jnp.zeros((comps, total), jnp.float32)
        for j in range(kp):
            one = jnp.where(of_kp == j, acc[j * comps : (j + 1) * comps], one)
        picked.append(one)
    ordered = jnp.dot(
        jnp.concatenate(picked, axis=0),
        order,
        precision=lax.Precision.HIGHEST,
        preferred_element_type=jnp.float32,
    )
    for k in range(k_count):
        for c in range(C):
            for part in range(parts):
                row = k * comps + c * C
                out[c * parts + part, k] = ordered[row : row + C, part * lanes : (part + 1) * lanes]


def contract(kp, k_count, parts, row, col, xs, slots):
    pair_count, comps, _ = xs[0].shape
    rows, cols = slots[0].shape
    n = len(slots)
    total = n * rows // k_count
    return pl.pallas_call(
        functools.partial(contract_kernel, kp, parts, n),
        out_shape=jax.ShapeDtypeStruct((C * parts, k_count, C, total // parts), jnp.float32),
        in_specs=[pl.BlockSpec(memory_space=pltpu.SMEM)] * 2 + [pl.BlockSpec(memory_space=pltpu.VMEM)] * (len(xs) + n),
        out_specs=pl.BlockSpec(memory_space=pltpu.VMEM),
        compiler_params=pltpu.CompilerParams(vmem_limit_bytes=14 << 20),
        cost_estimate=pl.CostEstimate(
            flops=2 * pair_count * comps * total * cols,
            bytes_accessed=2 * cols * (pair_count * comps + n * rows),
            transcendentals=0,
        ),
        name="contract",
    )(row, col, *xs, *slots)


def per_device(n, m, *args):
    return direct_kernel(n, m, *args)


def direct_kernel(n, m, conduction, valence, screened, pair_block):
    k_count, kp = pair_block.shape
    comps = conduction.shape[2]
    pair_count = k_count * kp
    local = valence.shape[2]
    cols = valence.shape[3]
    w = lax.axis_index("wrow").astype(jnp.int32)
    c = lax.axis_index("kblk").astype(jnp.int32)

    own = valence.reshape(pair_count * local, cols)
    slots = gather_valence(own, n, m)
    conds = [conduction]
    for i in range(1, m):
        conds.append(move(conduction, n, m, lambda w, c: w, lambda c: c ^ i))
    cond = jnp.concatenate(conds, axis=0).reshape(pair_count, comps, conduction.shape[3])
    me = (c * (k_count // m)).reshape(1)

    xs = []
    for piece in range(PIECES):
        xs.append(project(piece, PIECES, kp, pair_block, me, w.reshape(1), cond, screened))

    parts = n // C
    width = V * V // parts
    mine = contract(kp, k_count, parts, w.reshape(1), c.reshape(1), xs, slots)

    sent = mine.reshape(n * k_count, C, kp * width)
    got = lax.all_to_all(sent, AXES, 0, 0, tiled=True)
    total = got.reshape(n * m, k_count // m, C, kp, width // V, V).sum(0)
    return total.transpose(0, 3, 2, 1, 4).reshape(k_count // m, width // V, kp * C * V)


def solution(mesh):
    n, m = mesh.shape["wrow"], mesh.shape["kblk"]
    return jax.shard_map(
        functools.partial(per_device, n, m),
        mesh=mesh,
        in_specs=(
            P("kblk", None, None, "wrow"),
            P(None, None, "wrow", "kblk"),
            P(None, "wrow", "kblk"),
            P(),
        ),
        out_specs=P("kblk", "wrow", None),
        check_vma=False,
    )
```

```python
import functools

import jax
import jax.numpy as jnp
from jax import lax
from jax.experimental import pallas as pl
from jax.experimental.pallas import tpu as pltpu
from jax.sharding import PartitionSpec as P


C = 8
V = 8
AXES = ("wrow", "kblk")
GROUP = 3
SPANS = (3, 1, 2, 2)
AHEAD = 4


def pairs_of(n, m, to, across):
    return [(w * m + c, to(w, c) * m + across(c)) for w in range(n) for c in range(m)]


def move(array, n, m, to, across=lambda c: c):
    return lax.ppermute(array, AXES, pairs_of(n, m, to, across))


def gather_valence(own, n, m):
    to_a = lambda w, c: w ^ (1 if c % 2 == 0 else 2)
    to_b = lambda w, c: w ^ (2 if c % 2 == 0 else 1)
    near, far = (lambda w, c: w ^ 4), (lambda z: lambda w, c: w ^ (4 * z))
    base = [own]
    for z in range(1, n // 4):
        if z % 2 == 0:
            base.append(move(own, n, m, far(z)))
        else:
            base.append(move(base[z - 1], n, m, near))
    in_a, in_b, in_ab = [], [], []
    for z in range(n // 4):
        if z == 1:
            in_a.append(move(in_a[0], n, m, near))
            in_ab.append(move(in_ab[0], n, m, near))
        else:
            in_a.append(move(base[z], n, m, to_a))
            in_ab.append(move(in_a[z], n, m, to_b))
        in_b.append(move(base[z], n, m, to_b))
    return [slot for four in zip(base, in_a, in_b, in_ab) for slot in four]


def project_kernel(cap, kp, start, blocks, me, row_of, cond, w, x, lhs, slot, tiles, arrived):
    pair_count, comps, _ = cond.shape
    block_count, _, span = tiles.shape
    halves = arrived.shape[1]
    width = span // halves

    def fetch(q, half):
        return pltpu.make_async_copy(
            w.at[q, :, pl.ds(start + half * width, width)],
            tiles.at[q, :, pl.ds(half * width, width)],
            arrived.at[q, half],
        )

    for i in range(min(AHEAD, block_count * halves)):
        fetch(i // halves, i % halves).start()

    @pl.loop(0, block_count)
    def _(q):
        count = jnp.int32(0)
        for p in range(pair_count):
            match = blocks[p // kp, p % kp] == q

            @pl.when(match)
            def _():
                lhs[count] = cond[((p // kp) ^ me[0]) * kp + p % kp]
                slot[count] = p

            count = count + match.astype(jnp.int32)
        for half in range(halves):
            columns = pl.ds(half * width, width)
            fetch(q, half).wait()
            later, part_of = (half + AHEAD) // halves, (half + AHEAD) % halves

            @pl.when(q + later < block_count)
            def _():
                fetch(q + later, part_of).start()

            for first in range(0, cap, GROUP):
                size = min(GROUP, cap - first)

                @pl.when(count > first)
                def _():
                    rows = lhs[first : first + size].reshape(size * comps, lhs.shape[2])
                    part = jnp.dot(rows, tiles[q, :, columns], preferred_element_type=jnp.float32).astype(x.dtype)
                    for s in range(size):

                        @pl.when(count > first + s)
                        def _():
                            x[slot[first + s], :, columns] = part[s * comps : (s + 1) * comps]


def project(start, span, width, kp, blocks, me, row_of, cond, screened):
    pair_count, comps, rows = cond.shape
    block_count = screened.shape[0]
    cap = 3 * pair_count // 8
    halves = span // width
    return pl.pallas_call(
        functools.partial(project_kernel, cap, kp, start),
        out_shape=jax.ShapeDtypeStruct((pair_count, comps, span), cond.dtype),
        in_specs=[
            pl.BlockSpec(memory_space=pltpu.SMEM),
            pl.BlockSpec(memory_space=pltpu.SMEM),
            pl.BlockSpec(memory_space=pltpu.SMEM),
            pl.BlockSpec(memory_space=pltpu.VMEM),
            pl.BlockSpec(memory_space=pl.ANY),
        ],
        out_specs=pl.BlockSpec(memory_space=pltpu.VMEM),
        scratch_shapes=[
            pltpu.VMEM((cap, comps, rows), cond.dtype),
            pltpu.SMEM((cap,), jnp.int32),
            pltpu.VMEM((block_count, rows, span), screened.dtype),
            pltpu.SemaphoreType.DMA((block_count, halves)),
        ],
        compiler_params=pltpu.CompilerParams(vmem_limit_bytes=32 << 20),
        cost_estimate=pl.CostEstimate(
            flops=2 * pair_count * comps * rows * span,
            bytes_accessed=2 * (block_count * rows * span + pair_count * comps * (rows + span)),
            transcendentals=0,
        ),
        name="project",
    )(blocks, me, row_of, cond, screened)


def contract_kernel(kp, parts, n, row_of, col_of, *refs):
    xs, vale = refs[: -n - 1], refs[-n - 1 : -1]
    out = refs[-1]
    comps = xs[0].shape[1]
    k_count = xs[0].shape[0] // kp
    rows = vale[0].shape[0] // k_count
    total = n * rows
    local = rows // kp
    index = lax.broadcasted_iota(jnp.int32, (total, total), 0)
    slot, inner = index // rows, index % rows
    swapped = (slot // 4) * 4 + (slot % 2) * 2 + (slot // 2) % 2
    comp = (jnp.where(col_of[0] % 2 == 0, slot, swapped) ^ row_of[0]) * local + inner % local
    lanes = total // parts
    size = lanes // kp
    target = (comp // size) * lanes + (inner // local) * size + comp % size
    order = (target == lax.broadcasted_iota(jnp.int32, (total, total), 1)).astype(jnp.float32)
    of_kp = (lax.broadcasted_iota(jnp.int32, (comps, total), 1) // local) % kp

    picked = []
    for k in range(k_count):
        acc = jnp.zeros((kp * comps, total), jnp.float32)
        start = 0
        for x in xs:
            width = x.shape[2]
            left = x[k * kp : (k + 1) * kp].reshape(kp * comps, width)
            right = jnp.concatenate([v[k * rows : (k + 1) * rows, start : start + width] for v in vale], axis=0)
            start += width
            acc += lax.dot_general(left, right, (((1,), (1,)), ((), ())), preferred_element_type=jnp.float32)
        one = jnp.zeros((comps, total), jnp.float32)
        for j in range(kp):
            one = jnp.where(of_kp == j, acc[j * comps : (j + 1) * comps], one)
        picked.append(one)
    ordered = jnp.dot(
        jnp.concatenate(picked, axis=0),
        order,
        precision=lax.Precision.HIGHEST,
        preferred_element_type=jnp.float32,
    )
    for k in range(k_count):
        for c in range(C):
            for part in range(parts):
                row = k * comps + c * C
                out[c * parts + part, k] = ordered[row : row + C, part * lanes : (part + 1) * lanes]


def contract(kp, k_count, parts, row, col, xs, slots):
    pair_count, comps, _ = xs[0].shape
    rows, cols = slots[0].shape
    n = len(slots)
    total = n * rows // k_count
    return pl.pallas_call(
        functools.partial(contract_kernel, kp, parts, n),
        out_shape=jax.ShapeDtypeStruct((C * parts, k_count, C, total // parts), jnp.float32),
        in_specs=[pl.BlockSpec(memory_space=pltpu.SMEM)] * 2 + [pl.BlockSpec(memory_space=pltpu.VMEM)] * (len(xs) + n),
        out_specs=pl.BlockSpec(memory_space=pltpu.VMEM),
        compiler_params=pltpu.CompilerParams(vmem_limit_bytes=14 << 20),
        cost_estimate=pl.CostEstimate(
            flops=2 * pair_count * comps * total * cols,
            bytes_accessed=2 * cols * (pair_count * comps + n * rows),
            transcendentals=0,
        ),
        name="contract",
    )(row, col, *xs, *slots)


def per_device(n, m, *args):
    return direct_kernel(n, m, *args)


def direct_kernel(n, m, conduction, valence, screened, pair_block):
    k_count, kp = pair_block.shape
    comps = conduction.shape[2]
    pair_count = k_count * kp
    local = valence.shape[2]
    cols = valence.shape[3]
    w = lax.axis_index("wrow").astype(jnp.int32)
    c = lax.axis_index("kblk").astype(jnp.int32)

    own = valence.reshape(pair_count * local, cols)
    slots = gather_valence(own, n, m)
    conds = [conduction]
    for i in range(1, m):
        conds.append(move(conduction, n, m, lambda w, c: w, lambda c: c ^ i))
    cond = jnp.concatenate(conds, axis=0).reshape(pair_count, comps, conduction.shape[3])
    me = (c * (k_count // m)).reshape(1)

    xs = []
    unit = cols // sum(SPANS)
    for piece, size in enumerate(SPANS):
        start = unit * sum(SPANS[:piece])
        xs.append(project(start, unit * size, unit, kp, pair_block, me, w.reshape(1), cond, screened))

    parts = n // C
    width = V * V // parts
    mine = contract(kp, k_count, parts, w.reshape(1), c.reshape(1), xs, slots)

    sent = mine.reshape(n * k_count, C, kp * width)
    got = lax.all_to_all(sent, AXES, 0, 0, tiled=True)
    total = got.reshape(n * m, k_count // m, C, kp, width // V, V).sum(0)
    return total.transpose(0, 3, 2, 1, 4).reshape(k_count // m, width // V, kp * C * V)


def solution(mesh):
    n, m = mesh.shape["wrow"], mesh.shape["kblk"]
    return jax.shard_map(
        functools.partial(per_device, n, m),
        mesh=mesh,
        in_specs=(
            P("kblk", None, None, "wrow"),
            P(None, None, "wrow", "kblk"),
            P(None, "wrow", "kblk"),
            P(),
        ),
        out_specs=P("kblk", "wrow", None),
        check_vma=False,
    )
```
